512 devices in a mesh: rows: 128 (over y, z, core), users: 4 (over x).
Axes of the slice: x: 4, y: 4, z: 16, core: 2. Of those that a mesh axis runs over, the one named last changes fastest.
Arguments:
- old_basis: bfloat16 [49152, 4096], P('rows', 'users'), may hold values from -24 to 24
- new_atoms: bfloat16 [49152, 128], P('rows'), may hold values from -300 to 300
- user_residuals: bfloat16 [49152, 512], P('rows', 'users'), may hold values from -850 to 850
Outputs:
- new_block: bfloat16 [49152, 128], P('rows')
- updated_residuals: bfloat16 [49152, 512], P('rows', 'users')
The draws below stay inside these ranges and needn't reach their ends.
All inputs are finite; a program needn't handle non-finite values.
Results may differ from the reference program's by a relative error of at most 0.019.
Values may be sent and summed in bfloat16 or wider, within the bound.
A program may use at most 64 MiB of HBM per device.

```python
import math
import jax
import jax.numpy as jnp
from jax import lax

M_DEV = 384
K = 4096
B = 128
M = 49152
U = 512
N_ROWS = 128


def spread_pair(blocks, share):
    high = math.sqrt(blocks * share)
    rest = math.sqrt(blocks * (1.0 - share) / max(blocks - 1, 1))
    return (high, rest)


def basis_column(key, column):
    blocks = M // M_DEV
    high, rest = spread_pair(blocks, 0.25)
    owners = jax.random.permutation(jax.random.fold_in(key, 12), blocks)
    target = owners[column % blocks]
    column_key = jax.random.fold_in(jax.random.fold_in(key, 11), column)
    noise = jax.random.truncated_normal(column_key, -4.0, 4.0, (M,), jnp.float32)
    owner_row = jnp.arange(M, dtype=jnp.int32) // M_DEV
    return noise * jnp.where(owner_row == target, high, rest)


def fresh_atoms(key):
    blocks = M // M_DEV
    high, rest = spread_pair(blocks, 1.0 / 3.0)
    base_noise = jax.random.truncated_normal(jax.random.fold_in(key, 21), -4.0, 4.0, (M, B), jnp.float32)
    row_scale = jnp.exp(jax.random.uniform(jax.random.fold_in(key, 23), (M, 1), jnp.float32, 0.0, math.log(10.0)))
    mixed = base_noise + 0.5 * jnp.roll(base_noise, -1, axis=1) - 0.4 * jnp.roll(base_noise, -7, axis=1)
    col_scale = jnp.exp(jax.random.uniform(jax.random.fold_in(key, 24), (1, B), jnp.float32, 0.0, math.log(10.0)))
    owners = jax.random.permutation(jax.random.fold_in(key, 22), blocks)
    target = owners[jnp.arange(B, dtype=jnp.int32) % blocks]
    owner_row = jnp.arange(M, dtype=jnp.int32) // M_DEV
    factor = jnp.where(owner_row[:, None] == target[None, :], high, rest)
    return (0.036 * mixed * row_scale * col_scale * factor, row_scale)


def draw_old_basis(key, part):

    def one_column(column):
        return basis_column(key, column).astype(jnp.bfloat16)
    columns = lax.map(one_column, jnp.arange(K, dtype=jnp.int32))
    return columns.T


def draw_new_atoms(key, part):
    new_part, row_scale = fresh_atoms(key)
    picks = jax.random.randint(jax.random.fold_in(key, 31), (3, B), 0, K)
    signs = (jax.random.randint(jax.random.fold_in(key, 32), (3, B), 0, 2) * 2 - 1).astype(jnp.float32)
    amounts = jax.random.uniform(jax.random.fold_in(key, 33), (3, B), jnp.float32, 0.5, 1.0) * signs

    def one_column(column):
        return basis_column(key, column).astype(jnp.bfloat16).astype(jnp.float32)
    chosen = lax.map(one_column, picks.reshape(-1)).reshape(3, B, M)
    coherent = jnp.sum(chosen * amounts[:, :, None], axis=0)
    return (coherent.T + new_part).astype(jnp.bfloat16)


def draw_user_residuals(key, part):
    new_part, row_scale = fresh_atoms(key)
    picks = jax.random.randint(jax.random.fold_in(key, 41), (2, U), 0, B)
    signs = (jax.random.randint(jax.random.fold_in(key, 42), (2, U), 0, 2) * 2 - 1).astype(jnp.float32)
    amounts = jax.random.uniform(jax.random.fold_in(key, 43), (2, U), jnp.float32, 1.0, 2.0) * signs
    combined = jnp.take(new_part, picks[0], axis=1) * amounts[0][None, :] + jnp.take(new_part, picks[1], axis=1) * amounts[1][None, :]
    noise = jax.random.truncated_normal(jax.random.fold_in(key, 44), -4.0, 4.0, (M, U), jnp.float32)
    return (combined + 0.5 * noise * row_scale / 4.6).astype(jnp.bfloat16)


def setup_inputs(seed: int = 0) -> dict:
    arg_keys = jax.random.split(jax.random.key(seed), 4)
    old_basis = draw_old_basis(jax.random.fold_in(arg_keys[3], 71), 0)
    new_atoms = draw_new_atoms(jax.random.fold_in(arg_keys[3], 71), 0)
    user_residuals = draw_user_residuals(jax.random.fold_in(arg_keys[3], 71), 0)
    return {"old_basis": old_basis, "new_atoms": new_atoms, "user_residuals": user_residuals}


def column_sums(old_basis, remainder_low):
    basis_blocks = old_basis.reshape(N_ROWS, M_DEV, K)
    low_blocks = remainder_low.reshape(N_ROWS, M_DEV, B)

    def add_block(running, block_pair):
        product = jnp.einsum('rk,rb->kb', block_pair[0].astype(jnp.float32), block_pair[1].astype(jnp.float32))
        return (running + product, None)
    running, unused = lax.scan(add_block, jnp.zeros((K, B), jnp.float32), (basis_blocks, low_blocks))
    return running

def finish_block(remainder_low, gram_total, coupling_total, user_residuals, m_total):
    gram_matrix = gram_total / m_total
    factor_lower = jnp.linalg.cholesky(gram_matrix)
    identity = jnp.eye(gram_matrix.shape[0], dtype=jnp.float32)
    inverse = jax.scipy.linalg.solve_triangular(factor_lower, identity, lower=True)
    new_block = jnp.dot(remainder_low.astype(jnp.float32), inverse.T, precision=lax.Precision.HIGHEST).astype(jnp.bfloat16)
    weights_low = jnp.dot(inverse, coupling_total / m_total, precision=lax.Precision.HIGHEST).astype(jnp.bfloat16)
    updated = user_residuals.astype(jnp.float32) - jnp.dot(new_block.astype(jnp.float32), weights_low.astype(jnp.float32), preferred_element_type=jnp.float32)
    return (new_block, updated.astype(jnp.bfloat16))

def reference(old_basis, new_atoms, user_residuals):
    m_total = float(M)
    remainder = new_atoms.astype(jnp.float32)
    remainder_low = new_atoms
    for sweep_index in range(2):
        coef_low = (column_sums(old_basis, remainder_low) / m_total).astype(jnp.bfloat16)
        remainder = remainder - jnp.dot(old_basis.astype(jnp.float32), coef_low.astype(jnp.float32), preferred_element_type=jnp.float32)
        remainder_low = remainder.astype(jnp.bfloat16)
    gram_total = jnp.dot(remainder_low.T.astype(jnp.float32), remainder_low.astype(jnp.float32), preferred_element_type=jnp.float32)
    coupling_total = jnp.dot(remainder_low.T.astype(jnp.float32), user_residuals.astype(jnp.float32), preferred_element_type=jnp.float32)
    return finish_block(remainder_low, gram_total, coupling_total, user_residuals, m_total)
```

```python
import functools

import jax
import jax.numpy as jnp
from jax import lax
from jax.experimental import pallas as pl
from jax.experimental.pallas import tpu as pltpu
from jax.sharding import PartitionSpec as P

MESH = pl.DeviceIdType.MESH
F32 = jnp.float32
BF16 = jnp.bfloat16
Y, Z, CORES, X = 4, 16, 2, 4
STRIPE = 2
ROW_CHUNKS = 3


def place():
    row = lax.axis_index("rows")
    z = lax.rem(lax.div(row, CORES), Z)
    return (
        lax.div(row, CORES * Z),
        lax.div(z, STRIPE),
        lax.rem(z, STRIPE),
        lax.rem(row, CORES),
        lax.axis_index("users"),
    )


def device(y, pair, stripe, core, x):
    return ((y * Z + pair * STRIPE + stripe) * CORES + core, x)


def half_of(pair, stripe, core):
    pairs = Z // STRIPE
    return lax.rem(core + stripe + lax.div(2 * pair, pairs), 2)


def core_of(pair, stripe, half):
    pairs = Z // STRIPE
    return lax.rem(half + stripe + lax.div(2 * pair, pairs), 2)


def ring_order(n):
    return sorted(range(1, n), key=lambda d: -min(d, n - d))


def exchange_kernel(
    m_total,
    basis_hbm, atoms_hbm, users_hbm,
    low_out, sums_out,
    basis, atoms, users, low, remainder,
    mate_out, mate_in, patch_out, patch_in, far_out, far_in, own_piece, coef, image, own_image,
    gram_out, gram_in, gpatch_out, gpatch_in, gfar_in, gown, gpiece,
    load_sem,
    mate_s, mate_r, patch_s, patch_r, far_s, far_r, gather_s, gather_r, users_s, users_r,
):
    y, pair, stripe, core, x = place()
    pairs = Z // STRIPE
    owners = Y * STRIPE
    half = half_of(pair, stripe, core)
    owner = y * STRIPE + stripe
    atoms_b = atoms.shape[1]
    side = atoms_b // 2
    piece_rows = side // Y
    k_loc = basis.shape[1]
    piece_cols = k_loc // STRIPE
    rows = basis.shape[0]
    chunk = rows // ROW_CHUNKS
    gram_rows = side // owners

    def patch_device(shift):
        other = lax.rem(owner + shift, owners)
        other_y, other_stripe = lax.div(other, STRIPE), lax.rem(other, STRIPE)
        return other, other_y, other_stripe

    def same_half(shift):
        other, other_y, other_stripe = patch_device(shift)
        return device(other_y, pair, other_stripe, core_of(pair, other_stripe, half), x)

    def other_half(shift):
        other, other_y, other_stripe = patch_device(shift)
        return device(other_y, pair, other_stripe, core_of(pair, other_stripe, 1 - half), x)

    def far_device(shift):
        other = lax.rem(pair + shift, pairs)
        return device(y, other, stripe, core_of(other, stripe, half), x)

    def user_device(shift):
        return device(y, pair, stripe, core, lax.rem(x + shift, X))

    mate = device(y, pair, stripe, 1 - core, x)
    patch_order = sorted(range(1, owners), key=lambda d: -min(d, owners - d))
    far_order = ring_order(pairs)
    user_order = ring_order(X)

    barrier = pltpu.get_barrier_semaphore()
    peers = [mate]
    peers += [same_half(d) for d in patch_order] + [other_half(d) for d in patch_order]
    peers += [far_device(d) for d in far_order] + [user_device(d) for d in user_order]
    for peer in peers:
        pl.semaphore_signal(barrier, inc=1, device_id=peer, device_id_type=MESH)

    loads = [
        pltpu.make_async_copy(atoms_hbm, atoms, load_sem.at[0]),
        pltpu.make_async_copy(basis_hbm, basis, load_sem.at[1]),
        pltpu.make_async_copy(users_hbm, users, load_sem.at[2]),
    ]
    for load in loads:
        load.start()
    loads[0].wait()
    low[...] = atoms[...]
    remainder[...] = atoms[...].astype(F32)
    loads[1].wait()
    loads[2].wait()
    pl.semaphore_wait(barrier, len(peers))

    def remote(src, dst, send, recv, peer):
        return pltpu.make_async_remote_copy(
            src_ref=src, dst_ref=dst, send_sem=send, recv_sem=recv, device_id=peer, device_id_type=MESH
        )

    for sweep in range(2):
        sent = []
        turned = low[...].astype(F32).T.astype(BF16)
        halves = []
        mates = []
        for s in range(STRIPE):
            cols = pl.ds(s * piece_cols, piece_cols)
            product = jnp.dot(turned, basis[:, cols], preferred_element_type=F32)
            own_piece[:, cols] = product
            mate_out[sweep, :, cols] = own_piece[pl.ds(pl.multiple_of((1 - half) * side, side), side), cols].astype(BF16)
            copy = remote(
                mate_out.at[sweep, :, cols], mate_in.at[sweep, :, cols],
                mate_s.at[sweep, s], mate_r.at[sweep, s], mate,
            )
            copy.start()
            mates.append(copy)
        sent += mates
        for s in range(STRIPE):
            cols = pl.ds(s * piece_cols, piece_cols)
            mates[s].wait_recv()
            total = own_piece[pl.ds(pl.multiple_of(half * side, side), side), cols] + mate_in[sweep, :, cols].astype(F32)
            patch_out[sweep, :, cols] = total.astype(BF16)
        patch_copies = []
        for i, d in enumerate(patch_order):
            other, other_y, other_stripe = patch_device(d)
            src = patch_out.at[
                sweep,
                pl.ds(pl.multiple_of(other_y * piece_rows, piece_rows), piece_rows),
                pl.ds(pl.multiple_of(other_stripe * piece_cols, piece_cols), piece_cols),
            ]
            copy = remote(src, patch_in.at[sweep, owner], patch_s.at[sweep, i], patch_r.at[sweep, i], same_half(d))
            copy.start()
            patch_copies.append(copy)
        patch_in[sweep, owner] = patch_out[
            sweep,
            pl.ds(pl.multiple_of(y * piece_rows, piece_rows), piece_rows),
            pl.ds(pl.multiple_of(stripe * piece_cols, piece_cols), piece_cols),
        ]
        for copy in patch_copies:
            copy.wait_recv()
        sent += patch_copies
        total = patch_in[sweep, 0].astype(F32)
        for j in range(1, owners):
            total = total + patch_in[sweep, j].astype(F32)
        far_out[sweep] = total.astype(BF16)
        far_copies = []
        for i, d in enumerate(far_order):
            copy = remote(far_out.at[sweep], far_in.at[sweep, pair], far_s.at[sweep, i], far_r.at[sweep, i], far_device(d))
            copy.start()
            far_copies.append(copy)
        far_in[sweep, pair] = far_out[sweep]
        for copy in far_copies:
            copy.wait_recv()
        sent += far_copies
        total = far_in[sweep, 0].astype(F32)
        for j in range(1, pairs):
            total = total + far_in[sweep, j].astype(F32)
        mine = coef.at[
            sweep,
            pl.ds(pl.multiple_of(half * side + y * piece_rows, piece_rows), piece_rows),
            pl.ds(pl.multiple_of(stripe * piece_cols, piece_cols), piece_cols),
        ]
        mine[...] = (total / m_total).astype(BF16)
        gathers = []
        for i, d in enumerate(patch_order):
            for j, target in enumerate((same_half(d), other_half(d))):
                copy = remote(mine, mine, gather_s.at[sweep, 2 * i + j], gather_r.at[sweep, 2 * i + j], target)
                copy.start()
                gathers.append(copy)
        copy = remote(mine, mine, gather_s.at[sweep, 2 * owners - 2], gather_r.at[sweep, 2 * owners - 2], mate)
        copy.start()
        gathers.append(copy)
        for copy in gathers:
            copy.wait_recv()
        sent += gathers

        user_copies = []
        for c in range(ROW_CHUNKS):
            part = pl.ds(c * chunk, chunk)
            product = lax.dot_general(
                basis[part, :], coef[sweep], (((1,), (1,)), ((), ())), preferred_element_type=F32
            )
            own_image[sweep, part, :] = product.astype(BF16)
            for i, d in enumerate(user_order):
                copy = remote(
                    own_image.at[sweep, part, :], image.at[sweep, x, part, :],
                    users_s.at[sweep, c, i], users_r.at[sweep, c, i], user_device(d),
                )
                copy.start()
                user_copies.append(copy)
            image[sweep, x, part, :] = own_image[sweep, part, :]
        for c in range(ROW_CHUNKS):
            part = pl.ds(c * chunk, chunk)
            for copy in user_copies[c * len(user_order) : (c + 1) * len(user_order)]:
                copy.wait_recv()
            projected = image[sweep, 0, part, :].astype(F32)
            for j in range(1, X):
                projected = projected + image[sweep, j, part, :].astype(F32)
            left = remainder[part, :] - projected
            remainder[part, :] = left
            low[part, :] = left.astype(BF16)
        sent += user_copies
        for copy in sent:
            copy.wait_send()

    low_out[...] = low[...]
    turned = low[...].astype(F32).T.astype(BF16)
    gown[:, :atoms_b] = jnp.dot(turned, low[...], preferred_element_type=F32)
    gown[:, atoms_b:] = jnp.dot(turned, users[...], preferred_element_type=F32)
    gram_out[...] = gown[pl.ds(pl.multiple_of((1 - half) * side, side), side), :]
    sent = []
    copy = remote(gram_out, gram_in, mate_s.at[2, 0], mate_r.at[2, 0], mate)
    copy.start()
    sent.append(copy)
    copy.wait_recv()
    gpatch_out[...] = gown[pl.ds(pl.multiple_of(half * side, side), side), :] + gram_in[...]
    patch_copies = []
    for i, d in enumerate(patch_order):
        other, _, _ = patch_device(d)
        src = gpatch_out.at[pl.ds(pl.multiple_of(other * gram_rows, gram_rows), gram_rows), :]
        copy = remote(src, gpatch_in.at[owner], patch_s.at[2, i], patch_r.at[2, i], same_half(d))
        copy.start()
        patch_copies.append(copy)
    gpatch_in[owner] = gpatch_out[pl.ds(pl.multiple_of(owner * gram_rows, gram_rows), gram_rows), :]
    for copy in patch_copies:
        copy.wait_recv()
    sent += patch_copies
    total = gpatch_in[0]
    for j in range(1, owners):
        total = total + gpatch_in[j]
    gpiece[...] = total
    far_copies = []
    for i, d in enumerate(far_order):
        copy = remote(gpiece, gfar_in.at[pair], far_s.at[2, i], far_r.at[2, i], far_device(d))
        copy.start()
        far_copies.append(copy)
    gfar_in[pair] = gpiece[...]
    for copy in far_copies:
        copy.wait_recv()
    sent += far_copies
    total = gfar_in[0]
    for j in range(1, pairs):
        total = total + gfar_in[j]
    mine = sums_out.at[pl.ds(pl.multiple_of(half * side + owner * gram_rows, gram_rows), gram_rows), :]
    mine[...] = total / m_total
    gathers = []
    for i, d in enumerate(patch_order):
        for j, target in enumerate((same_half(d), other_half(d))):
            copy = remote(mine, mine, gather_s.at[2, 2 * i + j], gather_r.at[2, 2 * i + j], target)
            copy.start()
            gathers.append(copy)
    copy = remote(mine, mine, gather_s.at[2, 2 * owners - 2], gather_r.at[2, 2 * owners - 2], mate)
    copy.start()
    gathers.append(copy)
    for copy in gathers:
        copy.wait_recv()
    sent += gathers
    for copy in sent:
        copy.wait_send()


def exchange(old_basis, new_atoms, user_residuals, m_total):
    rows, k_loc = old_basis.shape
    b = new_atoms.shape[1]
    u = user_residuals.shape[1]
    owners, pairs = Y * STRIPE, Z // STRIPE
    side = b // 2
    piece = (side // Y, k_loc // STRIPE)
    gram_piece = (side // owners, b + u)
    dma = pltpu.SemaphoreType.DMA
    n_gather = 2 * owners - 1
    scratch = [
        pltpu.VMEM((rows, k_loc), BF16),
        pltpu.VMEM((rows, b), BF16),
        pltpu.VMEM((rows, u), BF16),
        pltpu.VMEM((rows, b), BF16),
        pltpu.VMEM((rows, b), F32),
        pltpu.VMEM((2, side, k_loc), BF16),
        pltpu.VMEM((2, side, k_loc), BF16),
        pltpu.VMEM((2, side, k_loc), BF16),
        pltpu.VMEM((2, owners, *piece), BF16),
        pltpu.VMEM((2, *piece), BF16),
        pltpu.VMEM((2, pairs, *piece), BF16),
        pltpu.VMEM((b, k_loc), F32),
        pltpu.VMEM((2, b, k_loc), BF16),
        pltpu.VMEM((2, X, rows, b), BF16),
        pltpu.VMEM((2, rows, b), BF16),
        pltpu.VMEM((side, b + u), F32),
        pltpu.VMEM((side, b + u), F32),
        pltpu.VMEM((side, b + u), F32),
        pltpu.VMEM((owners, *gram_piece), F32),
        pltpu.VMEM((pairs, *gram_piece), F32),
        pltpu.VMEM((b, b + u), F32),
        pltpu.VMEM(gram_piece, F32),
        dma((3,)),
        dma((3, STRIPE)), dma((3, STRIPE)),
        dma((3, max(owners - 1, 1))), dma((3, max(owners - 1, 1))),
        dma((3, max(pairs - 1, 1))), dma((3, max(pairs - 1, 1))),
        dma((3, n_gather)), dma((3, n_gather)),
        dma((2, ROW_CHUNKS, max(X - 1, 1))), dma((2, ROW_CHUNKS, max(X - 1, 1))),
    ]
    return pl.pallas_call(
        functools.partial(exchange_kernel, m_total),
        out_shape=(jax.ShapeDtypeStruct((rows, b), BF16), jax.ShapeDtypeStruct((b, b + u), F32)),
        in_specs=[pl.BlockSpec(memory_space=pl.ANY)] * 3,
        out_specs=(pl.BlockSpec(memory_space=pltpu.VMEM), pl.BlockSpec(memory_space=pltpu.VMEM)),
        scratch_shapes=scratch,
        compiler_params=pltpu.CompilerParams(collective_id=0, has_side_effects=True, vmem_limit_bytes=48 * 2**20),
    )(old_basis, new_atoms, user_residuals)


def finish_block(remainder_low, gram_matrix, coupling, user_residuals):
    factor_lower = jnp.linalg.cholesky(gram_matrix)
    identity = jnp.eye(gram_matrix.shape[0], dtype=F32)
    inverse = jax.scipy.linalg.solve_triangular(factor_lower, identity, lower=True)
    new_block = jnp.dot(remainder_low.astype(F32), inverse.T, precision=lax.Precision.HIGHEST).astype(BF16)
    weights_low = jnp.dot(inverse, coupling, precision=lax.Precision.HIGHEST).astype(BF16)
    updated = user_residuals.astype(F32) - jnp.dot(new_block, weights_low, preferred_element_type=F32)
    return (new_block, updated.astype(BF16))


def local(old_basis, new_atoms, user_residuals):
    m_total = float(old_basis.shape[0] * lax.axis_size("rows"))
    b = new_atoms.shape[1]
    remainder_low, sums = exchange(old_basis, new_atoms, user_residuals, m_total)
    return finish_block(remainder_low, sums[:, :b], sums[:, b:], user_residuals)


def solution(mesh):
    in_specs = (P("rows", "users"), P("rows", None), P("rows", "users"))
    out_specs = (P("rows", None), P("rows", "users"))
    return jax.shard_map(local, mesh=mesh, in_specs=in_specs, out_specs=out_specs, check_vma=False)
```

```python
import functools

import jax
import jax.numpy as jnp
from jax import lax
from jax.experimental import pallas as pl
from jax.experimental.pallas import tpu as pltpu
from jax.sharding import PartitionSpec as P

MESH = pl.DeviceIdType.MESH
F32 = jnp.float32
BF16 = jnp.bfloat16
Y, Z, CORES, X = 4, 16, 2, 4
STRIPE = 2
ROW_CHUNKS = 3


def place():
    row = lax.axis_index("rows")
    z = lax.rem(lax.div(row, CORES), Z)
    return (
        lax.div(row, CORES * Z),
        lax.div(z, STRIPE),
        lax.rem(z, STRIPE),
        lax.rem(row, CORES),
        lax.axis_index("users"),
    )


def device(y, pair, stripe, core, x):
    return ((y * Z + pair * STRIPE + stripe) * CORES + core, x)


def half_of(pair, stripe, core):
    pairs = Z // STRIPE
    return lax.rem(core + stripe + lax.div(2 * pair, pairs), 2)


def core_of(pair, stripe, half):
    pairs = Z // STRIPE
    return lax.rem(half + stripe + lax.div(2 * pair, pairs), 2)


def ring_order(n):
    return sorted(range(1, n), key=lambda d: -min(d, n - d))


def exchange_kernel(
    m_total,
    basis_hbm, atoms_hbm, users_hbm,
    low_out, sums_out,
    basis, atoms, users, low, remainder,
    mate_out, mate_in, patch_out, patch_in, far_out, far_in, own_piece, coef, image, own_image,
    gram_out, gram_in, gpatch_out, gpatch_in, gfar_in, gown, gpiece,
    load_sem,
    mate_s, mate_r, patch_s, patch_r, far_s, far_r, gather_s, gather_r, users_s, users_r,
):
    y, pair, stripe, core, x = place()
    pairs = Z // STRIPE
    owners = Y * STRIPE
    half = half_of(pair, stripe, core)
    owner = y * STRIPE + stripe
    atoms_b = atoms.shape[1]
    side = atoms_b // 2
    piece_rows = side // Y
    k_loc = basis.shape[1]
    piece_cols = k_loc // STRIPE
    rows = basis.shape[0]
    chunk = rows // ROW_CHUNKS
    gram_rows = side // owners

    def patch_device(shift):
        other = lax.rem(owner + shift, owners)
        other_y, other_stripe = lax.div(other, STRIPE), lax.rem(other, STRIPE)
        return other, other_y, other_stripe

    def same_half(shift):
        other, other_y, other_stripe = patch_device(shift)
        return device(other_y, pair, other_stripe, core_of(pair, other_stripe, half), x)

    def other_half(shift):
        other, other_y, other_stripe = patch_device(shift)
        return device(other_y, pair, other_stripe, core_of(pair, other_stripe, 1 - half), x)

    def far_device(shift):
        other = lax.rem(pair + shift, pairs)
        return device(y, other, stripe, core_of(other, stripe, half), x)

    def user_device(shift):
        return device(y, pair, stripe, core, lax.rem(x + shift, X))

    mate = device(y, pair, stripe, 1 - core, x)
    patch_order = sorted(range(1, owners), key=lambda d: -min(d, owners - d))
    far_order = ring_order(pairs)
    user_order = ring_order(X)

    barrier = pltpu.get_barrier_semaphore()
    peers = [mate]
    peers += [same_half(d) for d in patch_order] + [other_half(d) for d in patch_order]
    peers += [far_device(d) for d in far_order] + [user_device(d) for d in user_order]
    for peer in peers:
        pl.semaphore_signal(barrier, inc=1, device_id=peer, device_id_type=MESH)

    loads = [
        pltpu.make_async_copy(atoms_hbm, atoms, load_sem.at[0]),
        pltpu.make_async_copy(basis_hbm, basis, load_sem.at[1]),
        pltpu.make_async_copy(users_hbm, users, load_sem.at[2]),
    ]
    for load in loads:
        load.start()
    loads[0].wait()
    low[...] = atoms[...]
    remainder[...] = atoms[...].astype(F32)
    loads[1].wait()
    loads[2].wait()
    pl.semaphore_wait(barrier, len(peers))

    def remote(src, dst, send, recv, peer):
        return pltpu.make_async_remote_copy(
            src_ref=src, dst_ref=dst, send_sem=send, recv_sem=recv, device_id=peer, device_id_type=MESH
        )

    for sweep in range(2):
        sent = []
        turned = low[...].astype(F32).T.astype(BF16)
        halves = []
        mates = []
        for s in range(STRIPE):
            cols = pl.ds(s * piece_cols, piece_cols)
            product = jnp.dot(turned, basis[:, cols], preferred_element_type=F32)
            own_piece[:, cols] = product
            mate_out[sweep, :, cols] = own_piece[pl.ds(pl.multiple_of((1 - half) * side, side), side), cols].astype(BF16)
            copy = remote(
                mate_out.at[sweep, :, cols], mate_in.at[sweep, :, cols],
                mate_s.at[sweep, s], mate_r.at[sweep, s], mate,
            )
            copy.start()
            mates.append(copy)
        sent += mates
        for s in range(STRIPE):
            cols = pl.ds(s * piece_cols, piece_cols)
            mates[s].wait_recv()
            total = own_piece[pl.ds(pl.multiple_of(half * side, side), side), cols] + mate_in[sweep, :, cols].astype(F32)
            patch_out[sweep, :, cols] = total.astype(BF16)
        patch_copies = []
        for i, d in enumerate(patch_order):
            other, other_y, other_stripe = patch_device(d)
            src = patch_out.at[
                sweep,
                pl.ds(pl.multiple_of(other_y * piece_rows, piece_rows), piece_rows),
                pl.ds(pl.multiple_of(other_stripe * piece_cols, piece_cols), piece_cols),
            ]
            copy = remote(src, patch_in.at[sweep, owner], patch_s.at[sweep, i], patch_r.at[sweep, i], same_half(d))
            copy.start()
            patch_copies.append(copy)
        patch_in[sweep, owner] = patch_out[
            sweep,
            pl.ds(pl.multiple_of(y * piece_rows, piece_rows), piece_rows),
            pl.ds(pl.multiple_of(stripe * piece_cols, piece_cols), piece_cols),
        ]
        for copy in patch_copies:
            copy.wait_recv()
        sent += patch_copies
        total = patch_in[sweep, 0].astype(F32)
        for j in range(1, owners):
            total = total + patch_in[sweep, j].astype(F32)
        far_out[sweep] = total.astype(BF16)
        far_copies = []
        for i, d in enumerate(far_order):
            copy = remote(far_out.at[sweep], far_in.at[sweep, pair], far_s.at[sweep, i], far_r.at[sweep, i], far_device(d))
            copy.start()
            far_copies.append(copy)
        far_in[sweep, pair] = far_out[sweep]
        for copy in far_copies:
            copy.wait_recv()
        sent += far_copies
        total = far_in[sweep, 0].astype(F32)
        for j in range(1, pairs):
            total = total + far_in[sweep, j].astype(F32)
        mine = coef.at[
            sweep,
            pl.ds(pl.multiple_of(half * side + y * piece_rows, piece_rows), piece_rows),
            pl.ds(pl.multiple_of(stripe * piece_cols, piece_cols), piece_cols),
        ]
        mine[...] = (total / m_total).astype(BF16)
        gathers = []
        for i, d in enumerate(patch_order):
            for j, target in enumerate((same_half(d), other_half(d))):
                copy = remote(mine, mine, gather_s.at[sweep, 2 * i + j], gather_r.at[sweep, 2 * i + j], target)
                copy.start()
                gathers.append(copy)
        copy = remote(mine, mine, gather_s.at[sweep, 2 * owners - 2], gather_r.at[sweep, 2 * owners - 2], mate)
        copy.start()
        gathers.append(copy)
        for copy in gathers:
            copy.wait_recv()
        sent += gathers

        user_copies = []
        for c in range(ROW_CHUNKS):
            part = pl.ds(c * chunk, chunk)
            product = lax.dot_general(
                basis[part, :], coef[sweep], (((1,), (1,)), ((), ())), preferred_element_type=F32
            )
            own_image[sweep, part, :] = product.astype(BF16)
            for i, d in enumerate(user_order):
                copy = remote(
                    own_image.at[sweep, part, :], image.at[sweep, x, part, :],
                    users_s.at[sweep, c, i], users_r.at[sweep, c, i], user_device(d),
                )
                copy.start()
                user_copies.append(copy)
            image[sweep, x, part, :] = own_image[sweep, part, :]
        for c in range(ROW_CHUNKS):
            part = pl.ds(c * chunk, chunk)
            for copy in user_copies[c * len(user_order) : (c + 1) * len(user_order)]:
                copy.wait_recv()
            projected = image[sweep, 0, part, :].astype(F32)
            for j in range(1, X):
                projected = projected + image[sweep, j, part, :].astype(F32)
            left = remainder[part, :] - projected
            remainder[part, :] = left
            low[part, :] = left.astype(BF16)
        sent += user_copies
        for copy in sent:
            copy.wait_send()

    low_out[...] = low[...]
    turned = low[...].astype(F32).T.astype(BF16)
    gown[:, :atoms_b] = jnp.dot(turned, low[...], preferred_element_type=F32)
    gown[:, atoms_b:] = jnp.dot(turned, users[...], preferred_element_type=F32)
    gram_out[...] = gown[pl.ds(pl.multiple_of((1 - half) * side, side), side), :]
    sent = []
    copy = remote(gram_out, gram_in, mate_s.at[2, 0], mate_r.at[2, 0], mate)
    copy.start()
    sent.append(copy)
    copy.wait_recv()
    gpatch_out[...] = gown[pl.ds(pl.multiple_of(half * side, side), side), :] + gram_in[...]
    patch_copies = []
    for i, d in enumerate(patch_order):
        other, _, _ = patch_device(d)
        src = gpatch_out.at[pl.ds(pl.multiple_of(other * gram_rows, gram_rows), gram_rows), :]
        copy = remote(src, gpatch_in.at[owner], patch_s.at[2, i], patch_r.at[2, i], same_half(d))
        copy.start()
        patch_copies.append(copy)
    gpatch_in[owner] = gpatch_out[pl.ds(pl.multiple_of(owner * gram_rows, gram_rows), gram_rows), :]
    for copy in patch_copies:
        copy.wait_recv()
    sent += patch_copies
    total = gpatch_in[0]
    for j in range(1, owners):
        total = total + gpatch_in[j]
    gpiece[...] = total
    far_copies = []
    for i, d in enumerate(far_order):
        copy = remote(gpiece, gfar_in.at[pair], far_s.at[2, i], far_r.at[2, i], far_device(d))
        copy.start()
        far_copies.append(copy)
    gfar_in[pair] = gpiece[...]
    for copy in far_copies:
        copy.wait_recv()
    sent += far_copies
    total = gfar_in[0]
    for j in range(1, pairs):
        total = total + gfar_in[j]
    mine = sums_out.at[pl.ds(pl.multiple_of(half * side + owner * gram_rows, gram_rows), gram_rows), :]
    mine[...] = total / m_total
    gathers = []
    for i, d in enumerate(patch_order):
        for j, target in enumerate((same_half(d), other_half(d))):
            copy = remote(mine, mine, gather_s.at[2, 2 * i + j], gather_r.at[2, 2 * i + j], target)
            copy.start()
            gathers.append(copy)
    copy = remote(mine, mine, gather_s.at[2, 2 * owners - 2], gather_r.at[2, 2 * owners - 2], mate)
    copy.start()
    gathers.append(copy)
    for copy in gathers:
        copy.wait_recv()
    sent += gathers
    for copy in sent:
        copy.wait_send()


def exchange(old_basis, new_atoms, user_residuals, m_total):
    rows, k_loc = old_basis.shape
    b = new_atoms.shape[1]
    u = user_residuals.shape[1]
    owners, pairs = Y * STRIPE, Z // STRIPE
    side = b // 2
    piece = (side // Y, k_loc // STRIPE)
    gram_piece = (side // owners, b + u)
    dma = pltpu.SemaphoreType.DMA
    n_gather = 2 * owners - 1
    scratch = [
        pltpu.VMEM((rows, k_loc), BF16),
        pltpu.VMEM((rows, b), BF16),
        pltpu.VMEM((rows, u), BF16),
        pltpu.VMEM((rows, b), BF16),
        pltpu.VMEM((rows, b), F32),
        pltpu.VMEM((2, side, k_loc), BF16),
        pltpu.VMEM((2, side, k_loc), BF16),
        pltpu.VMEM((2, side, k_loc), BF16),
        pltpu.VMEM((2, owners, *piece), BF16),
        pltpu.VMEM((2, *piece), BF16),
        pltpu.VMEM((2, pairs, *piece), BF16),
        pltpu.VMEM((b, k_loc), F32),
        pltpu.VMEM((2, b, k_loc), BF16),
        pltpu.VMEM((2, X, rows, b), BF16),
        pltpu.VMEM((2, rows, b), BF16),
        pltpu.VMEM((side, b + u), F32),
        pltpu.VMEM((side, b + u), F32),
        pltpu.VMEM((side, b + u), F32),
        pltpu.VMEM((owners, *gram_piece), F32),
        pltpu.VMEM((pairs, *gram_piece), F32),
        pltpu.VMEM((b, b + u), F32),
        pltpu.VMEM(gram_piece, F32),
        dma((3,)),
        dma((3, STRIPE)), dma((3, STRIPE)),
        dma((3, max(owners - 1, 1))), dma((3, max(owners - 1, 1))),
        dma((3, max(pairs - 1, 1))), dma((3, max(pairs - 1, 1))),
        dma((3, n_gather)), dma((3, n_gather)),
        dma((2, ROW_CHUNKS, max(X - 1, 1))), dma((2, ROW_CHUNKS, max(X - 1, 1))),
    ]
    return pl.pallas_call(
        functools.partial(exchange_kernel, m_total),
        out_shape=(jax.ShapeDtypeStruct((rows, b), BF16), jax.ShapeDtypeStruct((b, b + u), F32)),
        in_specs=[pl.BlockSpec(memory_space=pl.ANY)] * 3,
        out_specs=(pl.BlockSpec(memory_space=pltpu.VMEM), pl.BlockSpec(memory_space=pltpu.VMEM)),
        scratch_shapes=scratch,
        compiler_params=pltpu.CompilerParams(collective_id=0, has_side_effects=True),
    )(old_basis, new_atoms, user_residuals)


def inverse_factor(work, n):
    step = 8
    for j in range(n // step):
        top = j * step
        block = work[top : top + step, :]
        wide = block.shape
        entry = {}
        for k in range(step):
            column = jnp.broadcast_to(block[:, top + k : top + k + 1], (step, n))
            for i in range(k, step):
                entry[i, k] = jnp.broadcast_to(column[i : i + 1, :], (step, n))
        left = [jnp.broadcast_to(block[i : i + 1, :n], (step, n)) for i in range(step)]
        right = [jnp.broadcast_to(block[i : i + 1, n:], (step, n)) for i in range(step)]
        for i in range(step):
            scale = lax.rsqrt(entry[i, i])
            left[i] = left[i] * scale
            right[i] = right[i] * scale
            factor = {k: entry[k, i] * scale for k in range(i + 1, step)}
            for k in range(i + 1, step):
                for m in range(i + 1, k + 1):
                    entry[k, m] = entry[k, m] - factor[k] * factor[m]
                left[k] = left[k] - factor[k] * left[i]
                right[k] = right[k] - factor[k] * right[i]
        line = lax.broadcasted_iota(jnp.int32, (step, n), 0)
        solved_left, solved_right = left[0], right[0]
        for i in range(1, step):
            solved_left = jnp.where(line == i, left[i], solved_left)
            solved_right = jnp.where(line == i, right[i], solved_right)
        work[top : top + step, n:] = solved_right
        rest = top + step
        if rest < n:
            solved = jnp.concatenate([solved_left, solved_right], axis=1)
            update = lax.dot_general(
                solved_left[:, rest:], solved, (((0,), (0,)), ((), ())),
                precision=lax.Precision.HIGHEST, preferred_element_type=F32,
            )
            work[rest:, :] = work[rest:, :] - update


def finish_kernel(low, sums, users, block_out, updated_out, work):
    n = low.shape[1]
    lines = lax.broadcasted_iota(jnp.int32, (n, n), 0)
    columns = lax.broadcasted_iota(jnp.int32, (n, n), 1)
    work[:, :n] = sums[:, :n]
    work[:, n:] = jnp.where(lines == columns, 1.0, 0.0)
    inverse_factor(work, n)
    inverse = work[:, n:]
    weights = jnp.dot(inverse, sums[:, n:], precision=lax.Precision.HIGHEST, preferred_element_type=F32).astype(BF16)
    new_block = lax.dot_general(
        low[...].astype(F32), inverse, (((1,), (1,)), ((), ())),
        precision=lax.Precision.HIGHEST, preferred_element_type=F32,
    ).astype(BF16)
    block_out[...] = new_block
    updated = users[...].astype(F32) - jnp.dot(new_block, weights, preferred_element_type=F32)
    updated_out[...] = updated.astype(BF16)


def finish(remainder_low, sums, user_residuals):
    rows, b = remainder_low.shape
    u = user_residuals.shape[1]
    return pl.pallas_call(
        finish_kernel,
        out_shape=(jax.ShapeDtypeStruct((rows, b), BF16), jax.ShapeDtypeStruct((rows, u), BF16)),
        in_specs=[pl.BlockSpec(memory_space=pltpu.VMEM)] * 3,
        out_specs=(pl.BlockSpec(memory_space=pltpu.VMEM), pl.BlockSpec(memory_space=pltpu.VMEM)),
        scratch_shapes=[pltpu.VMEM((b, 2 * b), F32)],
        compiler_params=pltpu.CompilerParams(vmem_limit_bytes=16 * 2**20),
    )(remainder_low, sums, user_residuals)


def local(old_basis, new_atoms, user_residuals):
    m_total = float(old_basis.shape[0] * lax.axis_size("rows"))
    remainder_low, sums = exchange(old_basis, new_atoms, user_residuals, m_total)
    return finish(remainder_low, sums, user_residuals)


def solution(mesh):
    in_specs = (P("rows", "users"), P("rows", None), P("rows", "users"))
    out_specs = (P("rows", None), P("rows", "users"))
    return jax.shard_map(local, mesh=mesh, in_specs=in_specs, out_specs=out_specs, check_vma=False)
```

```python
import functools

import jax
import jax.numpy as jnp
from jax import lax
from jax.experimental import pallas as pl
from jax.experimental.pallas import tpu as pltpu
from jax.sharding import PartitionSpec as P

MESH = pl.DeviceIdType.MESH
F32 = jnp.float32
BF16 = jnp.bfloat16
Y, Z, CORES, X = 4, 16, 2, 4
STRIPE = 2
ROW_CHUNKS = 3
GROUPS = 1


def place():
    row = lax.axis_index("rows")
    z = lax.rem(lax.div(row, CORES), Z)
    return (
        lax.div(row, CORES * Z),
        lax.div(z, STRIPE),
        lax.rem(z, STRIPE),
        lax.rem(row, CORES),
        lax.axis_index("users"),
    )


def device(y, pair, stripe, core, x):
    return ((y * Z + pair * STRIPE + stripe) * CORES + core, x)


def half_of(pair, stripe, core):
    pairs = Z // STRIPE
    return lax.rem(core + stripe + lax.div(2 * pair, pairs), 2)


def core_of(pair, stripe, half):
    pairs = Z // STRIPE
    return lax.rem(half + stripe + lax.div(2 * pair, pairs), 2)


def ring_order(n):
    return sorted(range(1, n), key=lambda d: -min(d, n - d))


def exchange_kernel(
    m_total,
    basis_hbm, atoms_hbm, users_hbm,
    low_out, sums_out,
    basis, atoms, users, low, remainder,
    mate_out, mate_in, patch_out, patch_in, far_out, far_in, own, coef, image, own_image, partial, meter, gmeter,
    gram_out, gram_in, gpatch_out, gpatch_in, gfar_in, gown, gpiece,
    load_sem, left_sem, right_sem,
    mate_s, mate_r, patch_s, patch_r, far_s, far_r, gather_s, gather_r, users_s, users_r,
    gmate_s, gmate_r, gpatch_s, gpatch_r, gfar_s, gfar_r, ggather_s, ggather_r,
):
    y, pair, stripe, core, x = place()
    pairs = Z // STRIPE
    owners = Y * STRIPE
    half = half_of(pair, stripe, core)
    owner = y * STRIPE + stripe
    atoms_b = atoms.shape[1]
    side = atoms_b // 2
    piece_rows = side // Y
    k_loc = basis.shape[1]
    piece_cols = k_loc // STRIPE
    rows = basis.shape[0]
    chunk = rows // ROW_CHUNKS
    gram_rows = side // owners

    def patch_device(shift):
        other = lax.rem(owner + shift, owners)
        other_y, other_stripe = lax.div(other, STRIPE), lax.rem(other, STRIPE)
        return other, other_y, other_stripe

    def same_half(shift):
        other, other_y, other_stripe = patch_device(shift)
        return device(other_y, pair, other_stripe, core_of(pair, other_stripe, half), x)

    def other_half(shift):
        other, other_y, other_stripe = patch_device(shift)
        return device(other_y, pair, other_stripe, core_of(pair, other_stripe, 1 - half), x)

    def far_device(shift):
        other = lax.rem(pair + shift, pairs)
        return device(y, other, stripe, core_of(other, stripe, half), x)

    def user_device(shift):
        return device(y, pair, stripe, core, lax.rem(x + shift, X))

    mate = device(y, pair, stripe, 1 - core, x)
    patch_order = sorted(range(1, owners), key=lambda d: -min(d, owners - d))
    far_order = ring_order(pairs)
    user_order = ring_order(X)

    barrier = pltpu.get_barrier_semaphore()
    peers = [mate]
    peers += [same_half(d) for d in patch_order] + [other_half(d) for d in patch_order]
    peers += [user_device(d) for d in user_order]
    left_reach, right_reach = pairs // 2, (pairs - 1) // 2
    if left_reach:
        peers.append(far_device(1))
    if right_reach:
        peers.append(far_device(pairs - 1))
    for peer in peers:
        pl.semaphore_signal(barrier, inc=1, device_id=peer, device_id_type=MESH)

    width = piece_cols // GROUPS

    def columns(g, stripe_index):
        return pl.ds(stripe_index * piece_cols + g * width, width)

    loads = [pltpu.make_async_copy(atoms_hbm, atoms, load_sem.at[0])]
    for g in range(GROUPS):
        for t in range(STRIPE):
            cols = columns(g, t)
            loads.append(pltpu.make_async_copy(basis_hbm.at[:, cols], basis.at[:, cols], load_sem.at[1 + g * STRIPE + t]))
    loads.append(pltpu.make_async_copy(users_hbm, users, load_sem.at[1 + GROUPS * STRIPE]))
    for load in loads:
        load.start()
    loads[0].wait()
    low[...] = atoms[...]
    remainder[...] = atoms[...].astype(F32)

    def pass_on(distance):
        if distance > 2:
            if left_reach >= distance - 1:
                pl.semaphore_wait(left_sem.at[distance - 3], 1)
            if right_reach >= distance - 1:
                pl.semaphore_wait(right_sem.at[distance - 3], 1)
        if left_reach >= distance:
            pl.semaphore_signal(left_sem.at[distance - 2], inc=1, device_id=far_device(1), device_id_type=MESH)
        if right_reach >= distance:
            pl.semaphore_signal(right_sem.at[distance - 2], inc=1, device_id=far_device(pairs - 1), device_id_type=MESH)

    def remote(src, dst, send, recv, peer):
        return pltpu.make_async_remote_copy(
            src_ref=src, dst_ref=dst, send_sem=send, recv_sem=recv, device_id=peer, device_id_type=MESH
        )

    def settle(like, count, sem):
        if count:
            pltpu.make_async_copy(like.at[pl.ds(0, count)], like.at[pl.ds(0, count)], sem).wait()

    piece_at = pl.ds(pl.multiple_of(y * piece_rows, piece_rows), piece_rows)
    keep_at = pl.ds(pl.multiple_of(half * side, side), side)
    give_at = pl.ds(pl.multiple_of((1 - half) * side, side), side)
    own_width = pl.ds(pl.multiple_of(stripe * width, width), width)

    for sweep in range(2):
        turned = low[...].astype(F32).T.astype(BF16)
        mates = []
        for g in range(GROUPS):
            for t in range(STRIPE):
                if sweep == 0:
                    loads[1 + g * STRIPE + t].wait()
                own[g, :, t * width : (t + 1) * width] = jnp.dot(
                    turned, basis[:, columns(g, t)], preferred_element_type=F32
                )
            mate_out[sweep, g] = own[g, give_at, :].astype(BF16)
            if sweep == 0 and g == 0:
                pl.semaphore_wait(barrier, len(peers))
                pass_on(2)
            copy = remote(mate_out.at[sweep, g], mate_in.at[sweep, g], mate_s.at[sweep, g], mate_r.at[sweep, g], mate)
            copy.start()
            mates.append(copy)
        patch_copies = []
        for g in range(GROUPS):
            mates[g].wait_recv()
            patch_out[sweep, g] = (own[g, keep_at, :] + mate_in[sweep, g].astype(F32)).astype(BF16)
            copies = []
            for i, d in enumerate(patch_order):
                other, other_y, other_stripe = patch_device(d)
                src = patch_out.at[
                    sweep, g,
                    pl.ds(pl.multiple_of(other_y * piece_rows, piece_rows), piece_rows),
                    pl.ds(pl.multiple_of(other_stripe * width, width), width),
                ]
                copy = remote(
                    src, patch_in.at[sweep, g, owner], patch_s.at[sweep, g], patch_r.at[sweep, g], same_half(d)
                )
                copy.start()
                copies.append(copy)
            patch_in[sweep, g, owner] = patch_out[sweep, g, piece_at, own_width]
            patch_copies.append(copies)
        if sweep == 0:
            pass_on(3)
        far_copies = []
        for g in range(GROUPS):
            if sweep == 0 and g == 0:
                pass_on(4)
            settle(meter, len(patch_order), patch_r.at[sweep, g])
            total = patch_in[sweep, g, 0].astype(F32)
            for j in range(1, owners):
                total = total + patch_in[sweep, g, j].astype(F32)
            far_out[sweep, g] = total.astype(BF16)
            if sweep == 0 and g == 0:
                pass_on(5)
            copies = []
            for i, d in enumerate(far_order):
                copy = remote(
                    far_out.at[sweep, g], far_in.at[sweep, g, pair], far_s.at[sweep, g], far_r.at[sweep, g],
                    far_device(d),
                )
                copy.start()
                copies.append(copy)
            far_in[sweep, g, pair] = far_out[sweep, g]
            far_copies.append(copies)
        gathers = []
        for g in range(GROUPS):
            settle(meter, len(far_order), far_r.at[sweep, g])
            total = far_in[sweep, g, 0].astype(F32)
            for j in range(1, pairs):
                total = total + far_in[sweep, g, j].astype(F32)
            mine = coef.at[
                sweep,
                pl.ds(pl.multiple_of(half * side + y * piece_rows, piece_rows), piece_rows),
                pl.ds(pl.multiple_of(stripe * piece_cols + g * width, width), width),
            ]
            mine[...] = (total / m_total).astype(BF16)
            targets = [mate]
            for d in patch_order:
                targets += [same_half(d), other_half(d)]
            targets = targets[1:] + targets[:1]
            copies = []
            for i, target in enumerate(targets):
                copy = remote(mine, mine, gather_s.at[sweep, g], gather_r.at[sweep, g], target)
                copy.start()
                copies.append(copy)
            gathers.append(copies)

        def image_part(rows_at, g):
            out = None
            for t in range(STRIPE):
                cols = columns(g, t)
                term = lax.dot_general(
                    basis[rows_at, cols], coef[sweep, :, cols], (((1,), (1,)), ((), ())), preferred_element_type=F32
                )
                out = term if out is None else out + term
            return out

        for g in range(GROUPS):
            settle(meter, len(gathers[g]), gather_r.at[sweep, g])
            if g < GROUPS - 1:
                for c in range(ROW_CHUNKS):
                    part = pl.ds(c * chunk, chunk)
                    term = image_part(part, g)
                    partial[part, :] = term if g == 0 else partial[part, :] + term
        user_copies = []
        for c in range(ROW_CHUNKS):
            part = pl.ds(c * chunk, chunk)
            product = image_part(part, GROUPS - 1)
            if GROUPS > 1:
                product = product + partial[part, :]
            own_image[sweep, part, :] = product.astype(BF16)
            for i, d in enumerate(user_order):
                copy = remote(
                    own_image.at[sweep, part, :], image.at[sweep, x, part, :],
                    users_s.at[sweep], users_r.at[sweep, c], user_device(d),
                )
                copy.start()
                user_copies.append(copy)
            image[sweep, x, part, :] = own_image[sweep, part, :]
        for c in range(ROW_CHUNKS):
            part = pl.ds(c * chunk, chunk)
            if user_order:
                arrived = image.at[sweep, pl.ds(0, len(user_order)), part, :]
                pltpu.make_async_copy(arrived, arrived, users_r.at[sweep, c]).wait()
            projected = image[sweep, 0, part, :].astype(F32)
            for j in range(1, X):
                projected = projected + image[sweep, j, part, :].astype(F32)
            left = remainder[part, :] - projected
            remainder[part, :] = left
            low[part, :] = left.astype(BF16)
        for g in range(GROUPS):
            mates[g].wait_send()
            settle(meter, len(patch_order), patch_s.at[sweep, g])
            settle(meter, len(far_order), far_s.at[sweep, g])
            settle(meter, len(gathers[g]), gather_s.at[sweep, g])
        if user_order:
            gone = image.at[sweep, pl.ds(0, len(user_order)), :, :]
            pltpu.make_async_copy(gone, gone, users_s.at[sweep]).wait()

    low_out[...] = low[...]
    loads[-1].wait()
    turned = low[...].astype(F32).T.astype(BF16)
    gown[:, :atoms_b] = jnp.dot(turned, low[...], preferred_element_type=F32)
    gown[:, atoms_b:] = jnp.dot(turned, users[...], preferred_element_type=F32)
    gram_out[...] = gown[pl.ds(pl.multiple_of((1 - half) * side, side), side), :]
    copy = remote(gram_out, gram_in, gmate_s.at[0], gmate_r.at[0], mate)
    copy.start()
    mate_copy = copy
    copy.wait_recv()
    gpatch_out[...] = gown[pl.ds(pl.multiple_of(half * side, side), side), :] + gram_in[...]
    patch_copies = []
    for i, d in enumerate(patch_order):
        other, _, _ = patch_device(d)
        src = gpatch_out.at[pl.ds(pl.multiple_of(other * gram_rows, gram_rows), gram_rows), :]
        copy = remote(src, gpatch_in.at[owner], gpatch_s.at[0], gpatch_r.at[0], same_half(d))
        copy.start()
        patch_copies.append(copy)
    gpatch_in[owner] = gpatch_out[pl.ds(pl.multiple_of(owner * gram_rows, gram_rows), gram_rows), :]
    settle(gmeter, len(patch_copies), gpatch_r.at[0])
    total = gpatch_in[0]
    for j in range(1, owners):
        total = total + gpatch_in[j]
    gpiece[...] = total
    far_copies = []
    for i, d in enumerate(far_order):
        copy = remote(gpiece, gfar_in.at[pair], gfar_s.at[0], gfar_r.at[0], far_device(d))
        copy.start()
        far_copies.append(copy)
    gfar_in[pair] = gpiece[...]
    settle(gmeter, len(far_copies), gfar_r.at[0])
    total = gfar_in[0]
    for j in range(1, pairs):
        total = total + gfar_in[j]
    mine = sums_out.at[pl.ds(pl.multiple_of(half * side + owner * gram_rows, gram_rows), gram_rows), :]
    mine[...] = total / m_total
    gathers = []
    for i, d in enumerate(patch_order):
        for j, target in enumerate((same_half(d), other_half(d))):
            copy = remote(mine, mine, ggather_s.at[0], ggather_r.at[0], target)
            copy.start()
            gathers.append(copy)
    copy = remote(mine, mine, ggather_s.at[0], ggather_r.at[0], mate)
    copy.start()
    gathers.append(copy)
    settle(gmeter, len(gathers), ggather_r.at[0])
    mate_copy.wait_send()
    settle(gmeter, len(patch_copies), gpatch_s.at[0])
    settle(gmeter, len(far_copies), gfar_s.at[0])
    settle(gmeter, len(gathers), ggather_s.at[0])


def exchange(old_basis, new_atoms, user_residuals, m_total):
    rows, k_loc = old_basis.shape
    b = new_atoms.shape[1]
    u = user_residuals.shape[1]
    owners, pairs = Y * STRIPE, Z // STRIPE
    side = b // 2
    width = k_loc // STRIPE // GROUPS
    piece = (side // Y, width)
    gram_piece = (side // owners, b + u)
    dma, signal = pltpu.SemaphoreType.DMA, pltpu.SemaphoreType.REGULAR
    scratch = [
        pltpu.VMEM((rows, k_loc), BF16),
        pltpu.VMEM((rows, b), BF16),
        pltpu.VMEM((rows, u), BF16),
        pltpu.VMEM((rows, b), BF16),
        pltpu.VMEM((rows, b), F32),
        pltpu.VMEM((2, GROUPS, side, STRIPE * width), BF16),
        pltpu.VMEM((2, GROUPS, side, STRIPE * width), BF16),
        pltpu.VMEM((2, GROUPS, side, STRIPE * width), BF16),
        pltpu.VMEM((2, GROUPS, owners, *piece), BF16),
        pltpu.VMEM((2, GROUPS, *piece), BF16),
        pltpu.VMEM((2, GROUPS, pairs, *piece), BF16),
        pltpu.VMEM((GROUPS, b, STRIPE * width), F32),
        pltpu.VMEM((2, b, k_loc), BF16),
        pltpu.VMEM((2, X, rows, b), BF16),
        pltpu.VMEM((2, rows, b), BF16),
        pltpu.VMEM((rows, b), F32),
        pltpu.VMEM((2 * owners, *piece), BF16),
        pltpu.VMEM((2 * owners, *gram_piece), F32),
        pltpu.VMEM((side, b + u), F32),
        pltpu.VMEM((side, b + u), F32),
        pltpu.VMEM((side, b + u), F32),
        pltpu.VMEM((owners, *gram_piece), F32),
        pltpu.VMEM((pairs, *gram_piece), F32),
        pltpu.VMEM((b, b + u), F32),
        pltpu.VMEM(gram_piece, F32),
        dma((2 + GROUPS * STRIPE,)), signal((3,)), signal((2,)),
        *[dma((2, GROUPS))] * 8,
        dma((2,)), dma((2, ROW_CHUNKS)),
        *[dma((1,))] * 8,
    ]
    return pl.pallas_call(
        functools.partial(exchange_kernel, m_total),
        out_shape=(jax.ShapeDtypeStruct((rows, b), BF16), jax.ShapeDtypeStruct((b, b + u), F32)),
        in_specs=[pl.BlockSpec(memory_space=pl.ANY)] * 3,
        out_specs=(pl.BlockSpec(memory_space=pltpu.VMEM), pl.BlockSpec(memory_space=pltpu.VMEM)),
        scratch_shapes=scratch,
        compiler_params=pltpu.CompilerParams(collective_id=0, has_side_effects=True),
    )(old_basis, new_atoms, user_residuals)


def inverse_factor(work, n):
    step = 8
    for j in range(n // step):
        top = j * step
        block = work[top : top + step, :]
        wide = block.shape
        entry = {}
        for k in range(step):
            column = jnp.broadcast_to(block[:, top + k : top + k + 1], (step, n))
            for i in range(k, step):
                entry[i, k] = jnp.broadcast_to(column[i : i + 1, :], (step, n))
        left = [jnp.broadcast_to(block[i : i + 1, :n], (step, n)) for i in range(step)]
        right = [jnp.broadcast_to(block[i : i + 1, n:], (step, n)) for i in range(step)]
        for i in range(step):
            scale = lax.rsqrt(entry[i, i])
            left[i] = left[i] * scale
            right[i] = right[i] * scale
            factor = {k: entry[k, i] * scale for k in range(i + 1, step)}
            for k in range(i + 1, step):
                for m in range(i + 1, k + 1):
                    entry[k, m] = entry[k, m] - factor[k] * factor[m]
                left[k] = left[k] - factor[k] * left[i]
                right[k] = right[k] - factor[k] * right[i]
        line = lax.broadcasted_iota(jnp.int32, (step, n), 0)
        solved_left, solved_right = left[0], right[0]
        for i in range(1, step):
            solved_left = jnp.where(line == i, left[i], solved_left)
            solved_right = jnp.where(line == i, right[i], solved_right)
        work[top : top + step, n:] = solved_right
        rest = top + step
        if rest < n:
            solved = jnp.concatenate([solved_left, solved_right], axis=1)
            update = lax.dot_general(
                solved_left[:, rest:], solved, (((0,), (0,)), ((), ())),
                precision=lax.Precision.HIGHEST, preferred_element_type=F32,
            )
            work[rest:, :] = work[rest:, :] - update


def finish_kernel(low, sums, users, block_out, updated_out, work):
    n = low.shape[1]
    lines = lax.broadcasted_iota(jnp.int32, (n, n), 0)
    columns = lax.broadcasted_iota(jnp.int32, (n, n), 1)
    work[:, :n] = sums[:, :n]
    work[:, n:] = jnp.where(lines == columns, 1.0, 0.0)
    inverse_factor(work, n)
    inverse = work[:, n:]
    weights = jnp.dot(inverse, sums[:, n:], precision=lax.Precision.HIGHEST, preferred_element_type=F32).astype(BF16)
    new_block = lax.dot_general(
        low[...].astype(F32), inverse, (((1,), (1,)), ((), ())),
        precision=lax.Precision.HIGHEST, preferred_element_type=F32,
    ).astype(BF16)
    block_out[...] = new_block
    updated = users[...].astype(F32) - jnp.dot(new_block, weights, preferred_element_type=F32)
    updated_out[...] = updated.astype(BF16)


def finish(remainder_low, sums, user_residuals):
    rows, b = remainder_low.shape
    u = user_residuals.shape[1]
    return pl.pallas_call(
        finish_kernel,
        out_shape=(jax.ShapeDtypeStruct((rows, b), BF16), jax.ShapeDtypeStruct((rows, u), BF16)),
        in_specs=[pl.BlockSpec(memory_space=pltpu.VMEM)] * 3,
        out_specs=(pl.BlockSpec(memory_space=pltpu.VMEM), pl.BlockSpec(memory_space=pltpu.VMEM)),
        scratch_shapes=[pltpu.VMEM((b, 2 * b), F32)],
        compiler_params=pltpu.CompilerParams(vmem_limit_bytes=16 * 2**20),
    )(remainder_low, sums, user_residuals)


def local(old_basis, new_atoms, user_residuals):
    m_total = float(old_basis.shape[0] * lax.axis_size("rows"))
    remainder_low, sums = exchange(old_basis, new_atoms, user_residuals, m_total)
    return finish(remainder_low, sums, user_residuals)


def solution(mesh):
    in_specs = (P("rows", "users"), P("rows", None), P("rows", "users"))
    out_specs = (P("rows", None), P("rows", "users"))
    return jax.shard_map(local, mesh=mesh, in_specs=in_specs, out_specs=out_specs, check_vma=False)
```

```python
import functools

import jax
import jax.numpy as jnp
from jax import lax
from jax.experimental import pallas as pl
from jax.experimental.pallas import tpu as pltpu
from jax.sharding import PartitionSpec as P

MESH = pl.DeviceIdType.MESH
F32 = jnp.float32
BF16 = jnp.bfloat16
Y, Z, CORES, X = 4, 16, 2, 4
STRIPE = 2
ROW_CHUNKS = 3
GROUPS = 1
STEP, SUB = 16, 8


def place():
    row = lax.axis_index("rows")
    z = lax.rem(lax.div(row, CORES), Z)
    return (
        lax.div(row, CORES * Z),
        lax.div(z, STRIPE),
        lax.rem(z, STRIPE),
        lax.rem(row, CORES),
        lax.axis_index("users"),
    )


def device(y, pair, stripe, core, x):
    return ((y * Z + pair * STRIPE + stripe) * CORES + core, x)


def half_of(pair, stripe, core):
    pairs = Z // STRIPE
    return lax.rem(core + stripe + lax.div(2 * pair, pairs), 2)


def core_of(pair, stripe, half):
    pairs = Z // STRIPE
    return lax.rem(half + stripe + lax.div(2 * pair, pairs), 2)


def ring_order(n):
    return sorted(range(1, n), key=lambda d: -min(d, n - d))


def inverse_factor(work, spread, n):
    step = STEP
    lane = lax.broadcasted_iota(jnp.int32, (step, n), 1)
    line = lax.broadcasted_iota(jnp.int32, (step, n), 0)
    for j in range(n // step):
        top = j * step
        rest = top + step
        block = work[top:rest, :]
        for k in range(step):
            spread[step * k : step * (k + 1), :] = jnp.broadcast_to(block[:, top + k : top + k + 1], (step, n))
        entry = {(i, k): spread[pl.ds(step * k + i, SUB, stride=0), :] for k in range(step) for i in range(k, step)}
        inside = (lane[:SUB] >= top) & (lane[:SUB] < rest)
        row = [
            jnp.where(inside, jnp.where(lane[:SUB] == top + i, 1.0, 0.0), work[pl.ds(top + i, SUB, stride=0), :])
            for i in range(step)
        ]
        for i in range(step):
            scale = lax.rsqrt(entry[i, i])
            row[i] = row[i] * scale
            factor = {k: entry[k, i] * scale for k in range(i + 1, step)}
            for k in range(i + 1, step):
                for m in range(i + 1, k + 1):
                    entry[k, m] = entry[k, m] - factor[k] * factor[m]
                row[k] = row[k] - factor[k] * row[i]
        parts = []
        for h in range(step // SUB):
            part = row[h * SUB]
            for i in range(1, SUB):
                part = jnp.where(line[:SUB] == i, row[h * SUB + i], part)
            parts.append(part)
        solved = parts[0] if len(parts) == 1 else jnp.concatenate(parts, axis=0)
        work[top:rest, :] = solved
        if rest < n:
            update = lax.dot_general(
                solved[:, rest:], solved, (((0,), (0,)), ((), ())),
                precision=lax.Precision.HIGHEST, preferred_element_type=F32,
            )
            wide = lax.broadcasted_iota(jnp.int32, (n - rest, n), 1)
            below = jnp.where((wide >= top) & (wide < rest), 0.0, work[rest:, :])
            work[rest:, :] = below - update


def exchange_kernel(
    m_total,
    basis_hbm, atoms_hbm, users_hbm,
    block_out, updated_out,
    basis, atoms, users, low, remainder,
    mate_out, mate_in, patch_out, patch_in, far_out, far_in, own, coef, image, own_image, partial, meter, gmeter, sums, factor, spread,
    gram_out, gram_in, gpatch_out, gpatch_in, gfar_in, gown, gpiece,
    load_sem, left_sem, right_sem,
    mate_s, mate_r, patch_s, patch_r, far_s, far_r, gather_s, gather_r, users_s, users_r,
    gmate_s, gmate_r, gpatch_s, gpatch_r, gfar_s, gfar_r, ggather_s, ggather_r,
):
    y, pair, stripe, core, x = place()
    pairs = Z // STRIPE
    owners = Y * STRIPE
    half = half_of(pair, stripe, core)
    owner = y * STRIPE + stripe
    atoms_b = atoms.shape[1]
    side = atoms_b // 2
    piece_rows = side // Y
    k_loc = basis.shape[1]
    piece_cols = k_loc // STRIPE
    rows = basis.shape[0]
    chunk = rows // ROW_CHUNKS
    gram_rows = side // owners

    def patch_device(shift):
        other = lax.rem(owner + shift, owners)
        other_y, other_stripe = lax.div(other, STRIPE), lax.rem(other, STRIPE)
        return other, other_y, other_stripe

    def same_half(shift):
        other, other_y, other_stripe = patch_device(shift)
        return device(other_y, pair, other_stripe, core_of(pair, other_stripe, half), x)

    def other_half(shift):
        other, other_y, other_stripe = patch_device(shift)
        return device(other_y, pair, other_stripe, core_of(pair, other_stripe, 1 - half), x)

    def far_device(shift):
        other = lax.rem(pair + shift, pairs)
        return device(y, other, stripe, core_of(other, stripe, half), x)

    def user_device(shift):
        return device(y, pair, stripe, core, lax.rem(x + shift, X))

    mate = device(y, pair, stripe, 1 - core, x)
    patch_order = sorted(range(1, owners), key=lambda d: -min(d, owners - d))
    far_order = ring_order(pairs)
    user_order = ring_order(X)

    barrier = pltpu.get_barrier_semaphore()
    peers = [mate]
    peers += [same_half(d) for d in patch_order] + [other_half(d) for d in patch_order]
    peers += [user_device(d) for d in user_order]
    left_reach, right_reach = pairs // 2, (pairs - 1) // 2
    if left_reach:
        peers.append(far_device(1))
    if right_reach:
        peers.append(far_device(pairs - 1))
    for peer in peers:
        pl.semaphore_signal(barrier, inc=1, device_id=peer, device_id_type=MESH)

    width = piece_cols // GROUPS

    def columns(g, stripe_index):
        return pl.ds(stripe_index * piece_cols + g * width, width)

    loads = [pltpu.make_async_copy(atoms_hbm, atoms, load_sem.at[0])]
    for g in range(GROUPS):
        for t in range(STRIPE):
            cols = columns(g, t)
            loads.append(pltpu.make_async_copy(basis_hbm.at[:, cols], basis.at[:, cols], load_sem.at[1 + g * STRIPE + t]))
    loads.append(pltpu.make_async_copy(users_hbm, users, load_sem.at[1 + GROUPS * STRIPE]))
    for load in loads:
        load.start()
    loads[0].wait()
    low[...] = atoms[...]
    remainder[...] = atoms[...].astype(F32)

    def pass_on(distance):
        if distance > 2:
            if left_reach >= distance - 1:
                pl.semaphore_wait(left_sem.at[distance - 3], 1)
            if right_reach >= distance - 1:
                pl.semaphore_wait(right_sem.at[distance - 3], 1)
        if left_reach >= distance:
            pl.semaphore_signal(left_sem.at[distance - 2], inc=1, device_id=far_device(1), device_id_type=MESH)
        if right_reach >= distance:
            pl.semaphore_signal(right_sem.at[distance - 2], inc=1, device_id=far_device(pairs - 1), device_id_type=MESH)

    def remote(src, dst, send, recv, peer):
        return pltpu.make_async_remote_copy(
            src_ref=src, dst_ref=dst, send_sem=send, recv_sem=recv, device_id=peer, device_id_type=MESH
        )

    def settle(like, count, sem):
        if count:
            pltpu.make_async_copy(like.at[pl.ds(0, count)], like.at[pl.ds(0, count)], sem).wait()

    piece_at = pl.ds(pl.multiple_of(y * piece_rows, piece_rows), piece_rows)
    keep_at = pl.ds(pl.multiple_of(half * side, side), side)
    give_at = pl.ds(pl.multiple_of((1 - half) * side, side), side)
    own_width = pl.ds(pl.multiple_of(stripe * width, width), width)

    for sweep in range(2):
        turned = low[...].astype(F32).T.astype(BF16)
        mates = []
        for g in range(GROUPS):
            for t in range(STRIPE):
                if sweep == 0:
                    loads[1 + g * STRIPE + t].wait()
                own[g, :, t * width : (t + 1) * width] = jnp.dot(
                    turned, basis[:, columns(g, t)], preferred_element_type=F32
                )
            mate_out[sweep, g] = own[g, give_at, :].astype(BF16)
            if sweep == 0 and g == 0:
                pl.semaphore_wait(barrier, len(peers))
                pass_on(2)
            copy = remote(mate_out.at[sweep, g], mate_in.at[sweep, g], mate_s.at[sweep, g], mate_r.at[sweep, g], mate)
            copy.start()
            mates.append(copy)
        patch_copies = []
        for g in range(GROUPS):
            mates[g].wait_recv()
            patch_out[sweep, g] = (own[g, keep_at, :] + mate_in[sweep, g].astype(F32)).astype(BF16)
            copies = []
            for i, d in enumerate(patch_order):
                other, other_y, other_stripe = patch_device(d)
                src = patch_out.at[
                    sweep, g,
                    pl.ds(pl.multiple_of(other_y * piece_rows, piece_rows), piece_rows),
                    pl.ds(pl.multiple_of(other_stripe * width, width), width),
                ]
                copy = remote(
                    src, patch_in.at[sweep, g, owner], patch_s.at[sweep, g], patch_r.at[sweep, g], same_half(d)
                )
                copy.start()
                copies.append(copy)
            patch_in[sweep, g, owner] = patch_out[sweep, g, piece_at, own_width]
            patch_copies.append(copies)
        if sweep == 0:
            pass_on(3)
        far_copies = []
        for g in range(GROUPS):
            if sweep == 0 and g == 0:
                pass_on(4)
            settle(meter, len(patch_order), patch_r.at[sweep, g])
            total = patch_in[sweep, g, 0].astype(F32)
            for j in range(1, owners):
                total = total + patch_in[sweep, g, j].astype(F32)
            far_out[sweep, g] = total.astype(BF16)
            if sweep == 0 and g == 0:
                pass_on(5)
            copies = []
            for i, d in enumerate(far_order):
                copy = remote(
                    far_out.at[sweep, g], far_in.at[sweep, g, pair], far_s.at[sweep, g], far_r.at[sweep, g],
                    far_device(d),
                )
                copy.start()
                copies.append(copy)
            far_in[sweep, g, pair] = far_out[sweep, g]
            far_copies.append(copies)
        gathers = []
        for g in range(GROUPS):
            settle(meter, len(far_order), far_r.at[sweep, g])
            total = far_in[sweep, g, 0].astype(F32)
            for j in range(1, pairs):
                total = total + far_in[sweep, g, j].astype(F32)
            mine = coef.at[
                sweep,
                pl.ds(pl.multiple_of(half * side + y * piece_rows, piece_rows), piece_rows),
                pl.ds(pl.multiple_of(stripe * piece_cols + g * width, width), width),
            ]
            mine[...] = (total / m_total).astype(BF16)
            targets = [mate]
            for d in patch_order:
                targets += [same_half(d), other_half(d)]
            targets = targets[1:] + targets[:1]
            copies = []
            for i, target in enumerate(targets):
                copy = remote(mine, mine, gather_s.at[sweep, g], gather_r.at[sweep, g], target)
                copy.start()
                copies.append(copy)
            gathers.append(copies)

        def image_part(rows_at, g):
            out = None
            for t in range(STRIPE):
                cols = columns(g, t)
                term = lax.dot_general(
                    basis[rows_at, cols], coef[sweep, :, cols], (((1,), (1,)), ((), ())), preferred_element_type=F32
                )
                out = term if out is None else out + term
            return out

        for g in range(GROUPS):
            settle(meter, len(gathers[g]), gather_r.at[sweep, g])
            if g < GROUPS - 1:
                for c in range(ROW_CHUNKS):
                    part = pl.ds(c * chunk, chunk)
                    term = image_part(part, g)
                    partial[part, :] = term if g == 0 else partial[part, :] + term
        user_copies = []
        for c in range(ROW_CHUNKS):
            part = pl.ds(c * chunk, chunk)
            product = image_part(part, GROUPS - 1)
            if GROUPS > 1:
                product = product + partial[part, :]
            own_image[sweep, part, :] = product.astype(BF16)
            for i, d in enumerate(user_order):
                copy = remote(
                    own_image.at[sweep, part, :], image.at[sweep, x, part, :],
                    users_s.at[sweep], users_r.at[sweep, c], user_device(d),
                )
                copy.start()
                user_copies.append(copy)
            image[sweep, x, part, :] = own_image[sweep, part, :]
        for c in range(ROW_CHUNKS):
            part = pl.ds(c * chunk, chunk)
            if user_order:
                arrived = image.at[sweep, pl.ds(0, len(user_order)), part, :]
                pltpu.make_async_copy(arrived, arrived, users_r.at[sweep, c]).wait()
            projected = image[sweep, 0, part, :].astype(F32)
            for j in range(1, X):
                projected = projected + image[sweep, j, part, :].astype(F32)
            left = remainder[part, :] - projected
            remainder[part, :] = left
            low[part, :] = left.astype(BF16)
        for g in range(GROUPS):
            mates[g].wait_send()
            settle(meter, len(patch_order), patch_s.at[sweep, g])
            settle(meter, len(far_order), far_s.at[sweep, g])
            settle(meter, len(gathers[g]), gather_s.at[sweep, g])
        if user_order:
            gone = image.at[sweep, pl.ds(0, len(user_order)), :, :]
            pltpu.make_async_copy(gone, gone, users_s.at[sweep]).wait()

    loads[-1].wait()
    turned = low[...].astype(F32).T.astype(BF16)
    gown[:, :atoms_b] = jnp.dot(turned, low[...], preferred_element_type=F32)
    gown[:, atoms_b:] = jnp.dot(turned, users[...], preferred_element_type=F32)
    gram_out[...] = gown[pl.ds(pl.multiple_of((1 - half) * side, side), side), :]
    copy = remote(gram_out, gram_in, gmate_s.at[0], gmate_r.at[0], mate)
    copy.start()
    mate_copy = copy
    copy.wait_recv()
    gpatch_out[...] = gown[pl.ds(pl.multiple_of(half * side, side), side), :] + gram_in[...]
    patch_copies = []
    for i, d in enumerate(patch_order):
        other, _, _ = patch_device(d)
        src = gpatch_out.at[pl.ds(pl.multiple_of(other * gram_rows, gram_rows), gram_rows), :]
        copy = remote(src, gpatch_in.at[owner], gpatch_s.at[0], gpatch_r.at[0], same_half(d))
        copy.start()
        patch_copies.append(copy)
    gpatch_in[owner] = gpatch_out[pl.ds(pl.multiple_of(owner * gram_rows, gram_rows), gram_rows), :]
    settle(gmeter, len(patch_copies), gpatch_r.at[0])
    total = gpatch_in[0]
    for j in range(1, owners):
        total = total + gpatch_in[j]
    gpiece[...] = total
    far_copies = []
    for i, d in enumerate(far_order):
        copy = remote(gpiece, gfar_in.at[pair], gfar_s.at[0], gfar_r.at[0], far_device(d))
        copy.start()
        far_copies.append(copy)
    gfar_in[pair] = gpiece[...]
    settle(gmeter, len(far_copies), gfar_r.at[0])
    total = gfar_in[0]
    for j in range(1, pairs):
        total = total + gfar_in[j]
    mine = sums.at[pl.ds(pl.multiple_of(half * side + owner * gram_rows, gram_rows), gram_rows), :]
    mine[...] = total / m_total
    gathers = []
    for i, d in enumerate(patch_order):
        for j, target in enumerate((same_half(d), other_half(d))):
            copy = remote(mine, mine, ggather_s.at[0], ggather_r.at[0], target)
            copy.start()
            gathers.append(copy)
    copy = remote(mine, mine, ggather_s.at[0], ggather_r.at[0], mate)
    copy.start()
    gathers.append(copy)
    settle(gmeter, len(gathers), ggather_r.at[0])
    factor[...] = sums[:, :atoms_b]
    inverse_factor(factor, spread, atoms_b)
    lines = lax.broadcasted_iota(jnp.int32, (atoms_b, atoms_b), 0)
    lanes = lax.broadcasted_iota(jnp.int32, (atoms_b, atoms_b), 1)
    inverse = jnp.where(lines >= lanes, factor[...], 0.0)
    weights = jnp.dot(
        inverse, sums[:, atoms_b:], precision=lax.Precision.HIGHEST, preferred_element_type=F32
    ).astype(BF16)
    new_block = lax.dot_general(
        low[...].astype(F32), inverse, (((1,), (1,)), ((), ())),
        precision=lax.Precision.HIGHEST, preferred_element_type=F32,
    ).astype(BF16)
    block_out[...] = new_block
    updated = users[...].astype(F32) - jnp.dot(new_block, weights, preferred_element_type=F32)
    updated_out[...] = updated.astype(BF16)
    mate_copy.wait_send()
    settle(gmeter, len(patch_copies), gpatch_s.at[0])
    settle(gmeter, len(far_copies), gfar_s.at[0])
    settle(gmeter, len(gathers), ggather_s.at[0])


def exchange(old_basis, new_atoms, user_residuals, m_total):
    rows, k_loc = old_basis.shape
    b = new_atoms.shape[1]
    u = user_residuals.shape[1]
    owners, pairs = Y * STRIPE, Z // STRIPE
    side = b // 2
    width = k_loc // STRIPE // GROUPS
    piece = (side // Y, width)
    gram_piece = (side // owners, b + u)
    dma, signal = pltpu.SemaphoreType.DMA, pltpu.SemaphoreType.REGULAR
    scratch = [
        pltpu.VMEM((rows, k_loc), BF16),
        pltpu.VMEM((rows, b), BF16),
        pltpu.VMEM((rows, u), BF16),
        pltpu.VMEM((rows, b), BF16),
        pltpu.VMEM((rows, b), F32),
        pltpu.VMEM((2, GROUPS, side, STRIPE * width), BF16),
        pltpu.VMEM((2, GROUPS, side, STRIPE * width), BF16),
        pltpu.VMEM((2, GROUPS, side, STRIPE * width), BF16),
        pltpu.VMEM((2, GROUPS, owners, *piece), BF16),
        pltpu.VMEM((2, GROUPS, *piece), BF16),
        pltpu.VMEM((2, GROUPS, pairs, *piece), BF16),
        pltpu.VMEM((GROUPS, b, STRIPE * width), F32),
        pltpu.VMEM((2, b, k_loc), BF16),
        pltpu.VMEM((2, X, rows, b), BF16),
        pltpu.VMEM((2, rows, b), BF16),
        pltpu.VMEM((rows, b), F32),
        pltpu.VMEM((2 * owners, *piece), BF16),
        pltpu.VMEM((2 * owners, *gram_piece), F32),
        pltpu.VMEM((b, b + u), F32),
        pltpu.VMEM((b, b), F32),
        pltpu.VMEM((STEP * STEP, b), F32),
        pltpu.VMEM((side, b + u), F32),
        pltpu.VMEM((side, b + u), F32),
        pltpu.VMEM((side, b + u), F32),
        pltpu.VMEM((owners, *gram_piece), F32),
        pltpu.VMEM((pairs, *gram_piece), F32),
        pltpu.VMEM((b, b + u), F32),
        pltpu.VMEM(gram_piece, F32),
        dma((2 + GROUPS * STRIPE,)), signal((3,)), signal((2,)),
        *[dma((2, GROUPS))] * 8,
        dma((2,)), dma((2, ROW_CHUNKS)),
        *[dma((1,))] * 8,
    ]
    return pl.pallas_call(
        functools.partial(exchange_kernel, m_total),
        out_shape=(jax.ShapeDtypeStruct((rows, b), BF16), jax.ShapeDtypeStruct((rows, u), BF16)),
        in_specs=[pl.BlockSpec(memory_space=pl.ANY)] * 3,
        out_specs=(pl.BlockSpec(memory_space=pltpu.VMEM), pl.BlockSpec(memory_space=pltpu.VMEM)),
        scratch_shapes=scratch,
        compiler_params=pltpu.CompilerParams(collective_id=0, has_side_effects=True, vmem_limit_bytes=55000 * 1024),
    )(old_basis, new_atoms, user_residuals)


def local(old_basis, new_atoms, user_residuals):
    m_total = float(old_basis.shape[0] * lax.axis_size("rows"))
    return exchange(old_basis, new_atoms, user_residuals, m_total)


def solution(mesh):
    in_specs = (P("rows", "users"), P("rows", None), P("rows", "users"))
    out_specs = (P("rows", None), P("rows", "users"))
    return jax.shard_map(local, mesh=mesh, in_specs=in_specs, out_specs=out_specs, check_vma=False)
```

```python
import functools

import jax
import jax.numpy as jnp
from jax import lax
from jax.experimental import pallas as pl
from jax.experimental.pallas import tpu as pltpu
from jax.sharding import PartitionSpec as P

MESH = pl.DeviceIdType.MESH
F32 = jnp.float32
BF16 = jnp.bfloat16
Y, Z, CORES, X = 4, 16, 2, 4
STRIPE = 2
ROW_CHUNKS = 3
GROUPS = 2
STEP, SUB = 16, 8


def place():
    row = lax.axis_index("rows")
    z = lax.rem(lax.div(row, CORES), Z)
    return (
        lax.div(row, CORES * Z),
        lax.div(z, STRIPE),
        lax.rem(z, STRIPE),
        lax.rem(row, CORES),
        lax.axis_index("users"),
    )


def device(y, pair, stripe, core, x):
    return ((y * Z + pair * STRIPE + stripe) * CORES + core, x)


def half_of(pair, stripe, core):
    pairs = Z // STRIPE
    return lax.rem(core + stripe + lax.div(2 * pair, pairs), 2)


def core_of(pair, stripe, half):
    pairs = Z // STRIPE
    return lax.rem(half + stripe + lax.div(2 * pair, pairs), 2)


def ring_order(n):
    return sorted(range(1, n), key=lambda d: -min(d, n - d))


def inverse_factor(work, spread, n):
    step = STEP
    lane = lax.broadcasted_iota(jnp.int32, (step, n), 1)
    line = lax.broadcasted_iota(jnp.int32, (step, n), 0)
    for j in range(n // step):
        top = j * step
        rest = top + step
        block = work[top:rest, :]
        for k in range(step):
            spread[step * k : step * (k + 1), :] = jnp.broadcast_to(block[:, top + k : top + k + 1], (step, n))
        entry = {(i, k): spread[pl.ds(step * k + i, SUB, stride=0), :] for k in range(step) for i in range(k, step)}
        inside = (lane[:SUB] >= top) & (lane[:SUB] < rest)
        row = [
            jnp.where(inside, jnp.where(lane[:SUB] == top + i, 1.0, 0.0), work[pl.ds(top + i, SUB, stride=0), :])
            for i in range(step)
        ]
        for i in range(step):
            scale = lax.rsqrt(entry[i, i])
            row[i] = row[i] * scale
            factor = {k: entry[k, i] * scale for k in range(i + 1, step)}
            for k in range(i + 1, step):
                for m in range(i + 1, k + 1):
                    entry[k, m] = entry[k, m] - factor[k] * factor[m]
                row[k] = row[k] - factor[k] * row[i]
        parts = []
        for h in range(step // SUB):
            part = row[h * SUB]
            for i in range(1, SUB):
                part = jnp.where(line[:SUB] == i, row[h * SUB + i], part)
            parts.append(part)
        solved = parts[0] if len(parts) == 1 else jnp.concatenate(parts, axis=0)
        work[top:rest, :] = solved
        if rest < n:
            update = lax.dot_general(
                solved[:, rest:], solved, (((0,), (0,)), ((), ())),
                precision=lax.Precision.HIGHEST, preferred_element_type=F32,
            )
            wide = lax.broadcasted_iota(jnp.int32, (n - rest, n), 1)
            below = jnp.where((wide >= top) & (wide < rest), 0.0, work[rest:, :])
            work[rest:, :] = below - update


def exchange_kernel(
    m_total,
    basis_hbm, atoms_hbm, users_hbm,
    both_out,
    basis, atoms, users, low, remainder,
    patch_out, patch_in, far_out, far_in, coef, image, own_image, partial, meter, gmeter, sums, factor, spread,
    gpatch_in, gfar_in, gown, gpiece,
    load_sem, left_sem, right_sem,
    patch_s, patch_r, far_s, far_r, gather_s, gather_r, users_s, users_r,
    gpatch_s, gpatch_r, gfar_s, gfar_r, ggather_s, ggather_r,
):
    y, pair, stripe, core, x = place()
    pairs = Z // STRIPE
    owners = Y * STRIPE
    half = half_of(pair, stripe, core)
    owner = y * STRIPE + stripe
    atoms_b = atoms.shape[1]
    side = atoms_b // 2
    piece_rows = side // Y
    k_loc = basis.shape[1]
    piece_cols = k_loc // STRIPE
    rows = basis.shape[0]
    chunk = rows // ROW_CHUNKS
    gram_rows = side // owners

    def patch_device(shift):
        other = lax.rem(owner + shift, owners)
        other_y, other_stripe = lax.div(other, STRIPE), lax.rem(other, STRIPE)
        return other, other_y, other_stripe

    def same_half(shift):
        other, other_y, other_stripe = patch_device(shift)
        return device(other_y, pair, other_stripe, core_of(pair, other_stripe, half), x)

    def other_half(shift):
        other, other_y, other_stripe = patch_device(shift)
        return device(other_y, pair, other_stripe, core_of(pair, other_stripe, 1 - half), x)

    def far_device(shift):
        other = lax.rem(pair + shift, pairs)
        return device(y, other, stripe, core_of(other, stripe, half), x)

    def user_device(shift):
        return device(y, pair, stripe, core, lax.rem(x + shift, X))

    patch_order = sorted(range(1, owners), key=lambda d: -min(d, owners - d))
    far_order = ring_order(pairs)
    user_order = ring_order(X)
    spots = owners * 2
    spot = owner * 2 + half
    patch = []
    for d in patch_order:
        other, other_y, other_stripe = patch_device(d)
        patch += [(half, other, other_y, other_stripe, same_half(d)), (1 - half, other, other_y, other_stripe, other_half(d))]
    patch.append((1 - half, owner, y, stripe, device(y, pair, stripe, 1 - core, x)))

    barrier = pltpu.get_barrier_semaphore()
    peers = [target for *_, target in patch]
    peers += [user_device(d) for d in user_order]
    left_reach, right_reach = pairs // 2, (pairs - 1) // 2
    if left_reach:
        peers.append(far_device(1))
    if right_reach:
        peers.append(far_device(pairs - 1))
    for peer in peers:
        pl.semaphore_signal(barrier, inc=1, device_id=peer, device_id_type=MESH)

    width = piece_cols // GROUPS

    def columns(g, stripe_index):
        return pl.ds(stripe_index * piece_cols + g * width, width)

    loads = [pltpu.make_async_copy(atoms_hbm, atoms, load_sem.at[0])]
    for g in range(GROUPS):
        for t in range(STRIPE):
            cols = columns(g, t)
            loads.append(pltpu.make_async_copy(basis_hbm.at[:, cols], basis.at[:, cols], load_sem.at[1 + g * STRIPE + t]))
    loads.append(pltpu.make_async_copy(users_hbm, users, load_sem.at[1 + GROUPS * STRIPE]))
    for load in loads:
        load.start()
    loads[0].wait()
    low[...] = atoms[...]
    remainder[...] = atoms[...].astype(F32)

    def pass_on(distance):
        if distance > 2:
            if left_reach >= distance - 1:
                pl.semaphore_wait(left_sem.at[distance - 3], 1)
            if right_reach >= distance - 1:
                pl.semaphore_wait(right_sem.at[distance - 3], 1)
        if left_reach >= distance:
            pl.semaphore_signal(left_sem.at[distance - 2], inc=1, device_id=far_device(1), device_id_type=MESH)
        if right_reach >= distance:
            pl.semaphore_signal(right_sem.at[distance - 2], inc=1, device_id=far_device(pairs - 1), device_id_type=MESH)

    def remote(src, dst, send, recv, peer):
        return pltpu.make_async_remote_copy(
            src_ref=src, dst_ref=dst, send_sem=send, recv_sem=recv, device_id=peer, device_id_type=MESH
        )

    def settle(like, count, sem):
        if count:
            pltpu.make_async_copy(like.at[pl.ds(0, count)], like.at[pl.ds(0, count)], sem).wait()

    own_width = pl.ds(pl.multiple_of(stripe * width, width), width)

    def piece_at(h, at_y):
        return pl.ds(pl.multiple_of(h * side + at_y * piece_rows, piece_rows), piece_rows)

    for sweep in range(2):
        turned = low[...].astype(F32).T.astype(BF16)
        for g in range(GROUPS):
            for t in range(STRIPE):
                if sweep == 0:
                    loads[1 + g * STRIPE + t].wait()
                patch_out[sweep, g, :, t * width : (t + 1) * width] = jnp.dot(
                    turned, basis[:, columns(g, t)], preferred_element_type=F32
                ).astype(BF16)
            if sweep == 0 and g == 0:
                pl.semaphore_wait(barrier, len(peers))
                pass_on(2)
            for h, _, at_y, at_stripe, target in patch:
                src = patch_out.at[
                    sweep, g, piece_at(h, at_y), pl.ds(pl.multiple_of(at_stripe * width, width), width)
                ]
                remote(
                    src, patch_in.at[sweep, g, spot], patch_s.at[sweep, g], patch_r.at[sweep, g], target
                ).start()
            patch_in[sweep, g, spot] = patch_out[sweep, g, piece_at(half, y), own_width]
        if sweep == 0:
            pass_on(3)
        far_copies = []
        for g in range(GROUPS):
            if sweep == 0 and g == 0:
                pass_on(4)
            settle(meter, len(patch), patch_r.at[sweep, g])
            total = patch_in[sweep, g, 0].astype(F32)
            for j in range(1, spots):
                total = total + patch_in[sweep, g, j].astype(F32)
            far_out[sweep, g] = total.astype(BF16)
            if sweep == 0 and g == 0:
                pass_on(5)
            copies = []
            for i, d in enumerate(far_order):
                copy = remote(
                    far_out.at[sweep, g], far_in.at[sweep, g, pair], far_s.at[sweep, g], far_r.at[sweep, g],
                    far_device(d),
                )
                copy.start()
                copies.append(copy)
            far_in[sweep, g, pair] = far_out[sweep, g]
            far_copies.append(copies)
        for g in range(GROUPS):
            settle(meter, len(far_order), far_r.at[sweep, g])
            total = far_in[sweep, g, 0].astype(F32)
            for j in range(1, pairs):
                total = total + far_in[sweep, g, j].astype(F32)
            mine = coef.at[
                sweep,
                piece_at(half, y),
                pl.ds(pl.multiple_of(stripe * piece_cols + g * width, width), width),
            ]
            mine[...] = (total / m_total).astype(BF16)
            for *_, target in patch:
                remote(mine, mine, gather_s.at[sweep, g], gather_r.at[sweep, g], target).start()

        def image_part(rows_at, g):
            out = None
            for t in range(STRIPE):
                cols = columns(g, t)
                term = lax.dot_general(
                    basis[rows_at, cols], coef[sweep, :, cols], (((1,), (1,)), ((), ())), preferred_element_type=F32
                )
                out = term if out is None else out + term
            return out

        for g in range(GROUPS):
            settle(meter, len(patch), gather_r.at[sweep, g])
            if g < GROUPS - 1:
                for c in range(ROW_CHUNKS):
                    part = pl.ds(c * chunk, chunk)
                    term = image_part(part, g)
                    partial[part, :] = term if g == 0 else partial[part, :] + term
        user_copies = []
        for c in range(ROW_CHUNKS):
            part = pl.ds(c * chunk, chunk)
            product = image_part(part, GROUPS - 1)
            if GROUPS > 1:
                product = product + partial[part, :]
            own_image[sweep, part, :] = product.astype(BF16)
            for i, d in enumerate(user_order):
                copy = remote(
                    own_image.at[sweep, part, :], image.at[sweep, x, part, :],
                    users_s.at[sweep], users_r.at[sweep, c], user_device(d),
                )
                copy.start()
                user_copies.append(copy)
            image[sweep, x, part, :] = own_image[sweep, part, :]
        for c in range(ROW_CHUNKS):
            part = pl.ds(c * chunk, chunk)
            if user_order:
                arrived = image.at[sweep, pl.ds(0, len(user_order)), part, :]
                pltpu.make_async_copy(arrived, arrived, users_r.at[sweep, c]).wait()
            projected = image[sweep, 0, part, :].astype(F32)
            for j in range(1, X):
                projected = projected + image[sweep, j, part, :].astype(F32)
            left = remainder[part, :] - projected
            remainder[part, :] = left
            low[part, :] = left.astype(BF16)

    loads[-1].wait()
    turned = low[...].astype(F32).T.astype(BF16)
    gown[:, :atoms_b] = jnp.dot(turned, low[...], preferred_element_type=F32)
    gown[:, atoms_b:] = jnp.dot(turned, users[...], preferred_element_type=F32)

    def gram_at(h, at_owner):
        return pl.ds(pl.multiple_of(h * side + at_owner * gram_rows, gram_rows), gram_rows)

    for h, other, _, _, target in patch:
        remote(gown.at[gram_at(h, other), :], gpatch_in.at[spot], gpatch_s.at[0], gpatch_r.at[0], target).start()
    gpatch_in[spot] = gown[gram_at(half, owner), :]
    settle(gmeter, len(patch), gpatch_r.at[0])
    total = gpatch_in[0]
    for j in range(1, spots):
        total = total + gpatch_in[j]
    gpiece[...] = total
    for d in far_order:
        remote(gpiece, gfar_in.at[pair], gfar_s.at[0], gfar_r.at[0], far_device(d)).start()
    gfar_in[pair] = gpiece[...]
    settle(gmeter, len(far_order), gfar_r.at[0])
    total = gfar_in[0]
    for j in range(1, pairs):
        total = total + gfar_in[j]
    mine = sums.at[gram_at(half, owner), :]
    mine[...] = total / m_total
    for *_, target in patch:
        remote(mine, mine, ggather_s.at[0], ggather_r.at[0], target).start()
    settle(gmeter, len(patch), ggather_r.at[0])
    factor[...] = sums[:, :atoms_b]
    inverse_factor(factor, spread, atoms_b)
    lines = lax.broadcasted_iota(jnp.int32, (atoms_b, atoms_b), 0)
    lanes = lax.broadcasted_iota(jnp.int32, (atoms_b, atoms_b), 1)
    inverse = jnp.where(lines >= lanes, factor[...], 0.0)
    weights = jnp.dot(
        inverse, sums[:, atoms_b:], precision=lax.Precision.HIGHEST, preferred_element_type=F32
    ).astype(BF16)
    turned_inverse = inverse.T
    high = turned_inverse.astype(BF16)
    middle = (turned_inverse - high.astype(F32)).astype(BF16)
    rest = (turned_inverse - high.astype(F32) - middle.astype(F32)).astype(BF16)
    twice = jnp.concatenate([low[...], low[...]], axis=1)
    small = jnp.dot(twice, jnp.concatenate([middle, rest], axis=0), preferred_element_type=F32)
    new_block = (small + jnp.dot(low[...], high, preferred_element_type=F32)).astype(BF16)
    both_out[:rows, :] = new_block
    updated = users[...].astype(F32) - jnp.dot(new_block, weights, preferred_element_type=F32)
    both_out[rows:, :] = updated.astype(BF16)

    for sweep in range(2):
        for g in range(GROUPS):
            settle(meter, len(patch), patch_s.at[sweep, g])
            settle(meter, len(far_order), far_s.at[sweep, g])
            settle(meter, len(patch), gather_s.at[sweep, g])
        if user_order:
            gone = image.at[sweep, pl.ds(0, len(user_order)), :, :]
            pltpu.make_async_copy(gone, gone, users_s.at[sweep]).wait()
    settle(gmeter, len(patch), gpatch_s.at[0])
    settle(gmeter, len(far_order), gfar_s.at[0])
    settle(gmeter, len(patch), ggather_s.at[0])


def exchange(old_basis, new_atoms, user_residuals, m_total):
    rows, k_loc = old_basis.shape
    b = new_atoms.shape[1]
    u = user_residuals.shape[1]
    owners, pairs = Y * STRIPE, Z // STRIPE
    side = b // 2
    width = k_loc // STRIPE // GROUPS
    piece = (side // Y, width)
    gram_piece = (side // owners, b + u)
    dma, signal = pltpu.SemaphoreType.DMA, pltpu.SemaphoreType.REGULAR
    scratch = [
        pltpu.VMEM((rows, k_loc), BF16),
        pltpu.VMEM((rows, b), BF16),
        pltpu.VMEM((rows, u), BF16),
        pltpu.VMEM((rows, b), BF16),
        pltpu.VMEM((rows, b), F32),
        pltpu.VMEM((2, GROUPS, b, STRIPE * width), BF16),
        pltpu.VMEM((2, GROUPS, 2 * owners, *piece), BF16),
        pltpu.VMEM((2, GROUPS, *piece), BF16),
        pltpu.VMEM((2, GROUPS, pairs, *piece), BF16),
        pltpu.VMEM((2, b, k_loc), BF16),
        pltpu.VMEM((2, X, rows, b), BF16),
        pltpu.VMEM((2, rows, b), BF16),
        pltpu.VMEM((rows, b), F32),
        pltpu.VMEM((2 * owners, *piece), BF16),
        pltpu.VMEM((2 * owners, *gram_piece), F32),
        pltpu.VMEM((b, b + u), F32),
        pltpu.VMEM((b, b), F32),
        pltpu.VMEM((STEP * STEP, b), F32),
        pltpu.VMEM((2 * owners, *gram_piece), F32),
        pltpu.VMEM((pairs, *gram_piece), F32),
        pltpu.VMEM((b, b + u), F32),
        pltpu.VMEM(gram_piece, F32),
        dma((2 + GROUPS * STRIPE,)), signal((3,)), signal((2,)),
        *[dma((2, GROUPS))] * 6,
        dma((2,)), dma((2, ROW_CHUNKS)),
        *[dma((1,))] * 6,
    ]
    return pl.pallas_call(
        functools.partial(exchange_kernel, m_total),
        out_shape=jax.ShapeDtypeStruct((2 * rows, b), BF16),
        in_specs=[pl.BlockSpec(memory_space=pl.ANY)] * 3,
        out_specs=pl.BlockSpec(memory_space=pltpu.VMEM),
        scratch_shapes=scratch,
        compiler_params=pltpu.CompilerParams(collective_id=0, has_side_effects=True, vmem_limit_bytes=48 * 2**20),
    )(*(pltpu.with_memory_space_constraint(v, pltpu.HBM) for v in (old_basis, new_atoms, user_residuals)))


def local(old_basis, new_atoms, user_residuals):
    m_total = float(old_basis.shape[0] * lax.axis_size("rows"))
    both = exchange(old_basis, new_atoms, user_residuals, m_total)
    rows = old_basis.shape[0]
    return both[:rows], both[rows:]


def solution(mesh):
    in_specs = (P("rows", "users"), P("rows", None), P("rows", "users"))
    out_specs = (P("rows", None), P("rows", "users"))
    return jax.shard_map(local, mesh=mesh, in_specs=in_specs, out_specs=out_specs, check_vma=False)
```
